128 devices in a mesh: row: 8 (over z, x_lo), col: 16 (over x_hi, y, core).
Axes of the slice: x: 4 (x_hi: 2, x_lo: 2; x = x_hi * 2 + x_lo), y: 4, z: 4, core: 2. Of those that a mesh axis runs over, the one named last changes fastest.
Arguments:
- t2_pairs: bfloat16 [8, 8, 16, 16, 64, 64], P('row', None, None, None, 'col'), may hold values from -6 to 6
- cycle_ints: bfloat16 [8192, 8192], P('row', 'col'), may hold values from -0.1875 to 0.1875
- eps_occ: float32 [8, 16], replicated, may hold values from -2 to -0.4
- eps_virt: float32 [8, 64], replicated, may hold values from 0.2 to 3
- occ_count: int32 [8], replicated, may hold values from 8 to 16, as said below
- virt_count: int32 [8], replicated, may hold values from 32 to 64, as said below
- window_irrep: int32 [1], replicated, may hold values from 0 to 7
Outputs:
- update: float32 [8192, 8192], P('row', 'col')
The draws below stay inside these ranges and needn't reach their ends.
Inputs may be any that keep to these rules, and one draw needn't show every extreme that they name: `occ_count`: at least half of the slots; one irrep fills all 16, and another holds exactly the least. `virt_count`: at least half of the slots; one irrep fills all 64, and another holds exactly the least.
All inputs are finite; a program needn't handle non-finite values.
Results may differ from the reference program's by a relative error of at most 0.0003.
Values may be sent and summed in bfloat16 or wider, within the bound.
A program may use at most 128 MiB of HBM per device.

```python
import jax
import jax.numpy as jnp
from jax import lax

NIRREP = 8
OCC_CAP = 16
VIR_CAP = 64
PH_DIM = 8192


def capped_counts(key, capacity):
    key_one, key_two, key_three = jax.random.split(jax.random.fold_in(key, 7), 3)
    least = max(capacity // 2, 1)
    counts = jax.random.randint(key_one, (NIRREP,), least, capacity + 1)
    fullest = jax.random.randint(key_two, (), 0, NIRREP)
    offset = jax.random.randint(key_three, (), 1, NIRREP)
    emptiest = (fullest + offset) % NIRREP
    irreps = jnp.arange(NIRREP)
    counts = jnp.where(irreps == fullest, capacity, counts)
    counts = jnp.where(irreps == emptiest, least, counts)
    return counts.astype(jnp.int32)


def draw_occ_count(key, part):
    return capped_counts(jax.random.fold_in(key, 11), OCC_CAP)


def draw_virt_count(key, part):
    return capped_counts(jax.random.fold_in(key, 23), VIR_CAP)


def block_levels(key, dims, pieces, low, largest):
    level, own = 1.0, jax.random.fold_in(key, 6)
    for position, shards_of in pieces:
        steps = jnp.exp(jax.random.uniform(jax.random.fold_in(own, position), (shards_of,), jnp.float32, low / len(pieces), largest / len(pieces)))
        level = level * jnp.repeat(steps, dims[position] // shards_of).reshape([-1 if axis == position else 1 for axis in range(len(dims))])
    return level


def gaussian(stream_key, shape, deviation, limit, shards=(), kind=jnp.bfloat16):
    result = deviation * jax.random.normal(stream_key, shape, jnp.float32)
    if shards:
        result = result * block_levels(stream_key, shape, shards, -0.22, 0.18)
    return jnp.clip(result, -limit, limit).astype(kind)


def setup_inputs(seed: int = 0) -> dict:
    key_list = jax.random.split(jax.random.key(seed), 8)
    return {
        "t2_pairs": gaussian(key_list[0], (NIRREP, NIRREP, OCC_CAP, OCC_CAP, VIR_CAP, VIR_CAP), 1.0, 6.0, ((0, 8), (4, 16))),
        "cycle_ints": gaussian(key_list[1], (PH_DIM, PH_DIM), (PH_DIM // 8) ** -0.5, 0.1875, ((0, 8), (1, 16))),
        "eps_occ": jnp.clip(jax.random.uniform(key_list[2], (NIRREP, OCC_CAP), jnp.float32, -2.0, -0.4), -2.0, -0.4),
        "eps_virt": jnp.clip(jax.random.uniform(key_list[3], (NIRREP, VIR_CAP), jnp.float32, 0.2, 3.0), 0.2, 3.0),
        "occ_count": draw_occ_count(jax.random.fold_in(key_list[7], 71), 0),
        "virt_count": draw_virt_count(jax.random.fold_in(key_list[7], 71), 0),
        "window_irrep": jax.random.randint(key_list[6], (1,), 0, 8).astype(jnp.int32),
    }


def ph_vectors(eps_occ, eps_virt, occ_count, virt_count, window_irrep):
    irreps = jnp.arange(NIRREP, dtype=jnp.int32)
    partner = jnp.bitwise_xor(irreps, window_irrep[0])
    onehot = (partner[:, None] == irreps[None, :])
    virt_rows = jnp.dot(onehot.astype(jnp.float32), eps_virt, precision=lax.Precision.HIGHEST)
    virt_live = jnp.sum(jnp.where(onehot, virt_count[None, :], 0), axis=1)
    energy = eps_occ[:, None, :] - virt_rows[:, :, None]
    slots_occ = jnp.arange(OCC_CAP, dtype=jnp.int32)
    slots_virt = jnp.arange(VIR_CAP, dtype=jnp.int32)
    live = (slots_occ[None, None, :] < occ_count[:, None, None]) & (slots_virt[None, :, None] < virt_live[:, None, None])
    return energy.reshape(-1), live.reshape(-1)


def reference(t2_pairs, cycle_ints, eps_occ, eps_virt, occ_count, virt_count, window_irrep):
    energy, live = ph_vectors(eps_occ, eps_virt, occ_count, virt_count, window_irrep)
    amps = jnp.transpose(t2_pairs, (0, 4, 2, 1, 5, 3)).reshape(PH_DIM, PH_DIM)
    both = live[:, None] & live[None, :]
    amps = jnp.where(both, amps, jnp.zeros_like(amps)).astype(jnp.bfloat16)
    cycle = jnp.dot(cycle_ints, amps, preferred_element_type=jnp.float32)
    denom = energy[:, None] + energy[None, :]
    return jnp.where(both, cycle / denom, jnp.float32(0.0))
```

```python
import jax
import jax.numpy as jnp
from jax import lax
from jax.experimental import pallas as pl
from jax.experimental.pallas import tpu as pltpu
from jax.sharding import PartitionSpec as P

MESH = pl.DeviceIdType.MESH
NIRREP = 8
OCC = 16
VIR = 64
BLOCK = 512
ROWS = 1024
HALF = 512
N_SENDS = 80


def kernel(x_ref, w_ref, eocc, evirt, nocc, nvirt, window, out_ref,
           wbuf, tbuf, abuf, s32, lhs, inv, w_rs, s_rs, t_rs, a_rs, ss, loc):
    row = lax.axis_index("row")
    col = lax.axis_index("col")
    z, xl = row // 2, row % 2
    xh, y, core = col // 8, (col // 2) % 4, col % 2
    g = window[0]

    def col_of(a, b, k):
        return a * 8 + b * 2 + k

    y_up = (row, col_of(xh, (y + 1) % 4, core))
    y_dn = (row, col_of(xh, (y + 3) % 4, core))
    x_far = (row, col_of(1 - xh, y, core))
    sibling = (row, col_of(xh, y, 1 - core))
    z_up = (((z + 1) % 4) * 2 + xl, col)
    z_dn = (((z + 3) % 4) * 2 + xl, col)
    x_near = (z * 2 + 1 - xl, col)
    a2a = [(dx, dy, dk) for dx in range(2) for dy in range(4) for dk in range(2)
           if (dx, dy, dk) != (0, 0, 0)]

    def peer(d):
        return col_of((xh + d[0]) % 2, (y + d[1]) % 4, (core + d[2]) % 2)

    barrier = pltpu.get_barrier_semaphore()
    for d in a2a:
        pl.semaphore_signal(barrier, inc=1, device_id=(row, peer(d)), device_id_type=MESH)
    for dev in (z_up, z_dn, x_near):
        pl.semaphore_signal(barrier, inc=1, device_id=dev, device_id_type=MESH)

    mine = pltpu.make_async_copy(w_ref, wbuf.at[xh * 4 + y, core], loc)
    mine.start()

    rid = lax.broadcasted_iota(jnp.int32, (64, 128), 0)
    lane = lax.broadcasted_iota(jnp.int32, (64, 128), 1)
    live_src = (rid % OCC < nocc[row]) & (col * 4 + rid // OCC < nvirt[row ^ g])

    def prepare(h2, _):
        for p in range(OCC):
            s32[pl.ds(p, 64, stride=OCC), 0:VIR] = x_ref[h2, p].astype(jnp.float32)
        for pair in range(8):
            lo = s32[pl.ds(pair * 128, 64), :]
            hi = pltpu.roll(s32[pl.ds(pair * 128 + 64, 64), :], 64, 1)
            both = jnp.where(live_src, jnp.where(lane < VIR, lo, hi), 0.0)
            lhs[pl.ds(h2 * 64, 64), pl.ds(pair * 128, 128)] = both.astype(jnp.bfloat16)
        return 0

    lax.fori_loop(0, NIRREP, prepare, 0)
    mine.wait()
    pl.semaphore_wait(barrier, len(a2a) + 3)

    sends = []

    def push(src, dst, rsem, dev):
        cp = pltpu.make_async_remote_copy(
            src_ref=src, dst_ref=dst, send_sem=ss.at[len(sends)], recv_sem=rsem,
            device_id=dev, device_id_type=MESH)
        cp.start()
        sends.append(cp)

    def arrived(ref, rsem):
        pltpu.make_async_remote_copy(
            src_ref=ref, dst_ref=ref, send_sem=ss.at[N_SENDS - 1], recv_sem=rsem,
            device_id=sibling, device_id_type=MESH).wait_recv()

    def wslot(da, db, j, k):
        return wbuf.at[((xh + da) % 2) * 4 + (y + db) % 4, k, pl.ds(j * HALF, HALF)]

    def w_up(da, db, j):
        s = wslot(da, db, j, core)
        push(s, s, w_rs.at[da, (db + 3) % 4, j], y_up)

    def w_dn(da, db, j):
        s = wslot(da, db, j, core)
        push(s, s, w_rs.at[da, (db + 1) % 4, j], y_dn)

    def w_far(da, db, j):
        s = wslot(da, db, j, core)
        push(s, s, w_rs.at[1 - da, db, j], x_far)

    def w_sib(da, db, j):
        s = wslot(da, db, j, core)
        push(s, s, s_rs.at[da, db, j], sibling)

    def w_in(da, db, j):
        arrived(wslot(da, db, j, core), w_rs.at[da, db, j])
        w_sib(da, db, j)

    def tslot(da, db, j):
        return tbuf.at[((z + db) % 4) * 2 + (xl + da) % 2, pl.ds(((xh + j) % 2) * HALF, HALF)]

    def t_up(da, db, j):
        s = tslot(da, db, j)
        push(s, s, t_rs.at[da, (db + 3) % 4, j], z_up)

    def t_dn(da, db, j):
        s = tslot(da, db, j)
        push(s, s, t_rs.at[da, (db + 1) % 4, j], z_dn)

    def t_near(da, db, j):
        s = tslot(da, db, j)
        push(s, s, t_rs.at[1 - da, db, j], x_near)

    def t_in(da, db, j):
        arrived(tslot(da, db, j), t_rs.at[da, db, j])

    w_up(0, 0, 0)
    w_dn(0, 0, 1)
    w_far(0, 0, 0)
    w_far(0, 0, 1)
    w_sib(0, 0, 0)
    w_sib(0, 0, 1)

    src = lax.broadcasted_iota(jnp.int32, (1024, 256), 0)
    dst = lax.broadcasted_iota(jnp.int32, (1024, 256), 1)
    code = (src % VIR) * OCC + src // VIR
    for n in range(4):
        onehot = jnp.where(code == dst + n * 256, 1.0, 0.0).astype(jnp.bfloat16)
        moved = jnp.dot(lhs[...], onehot, preferred_element_type=jnp.float32).astype(jnp.bfloat16)
        for h2 in range(NIRREP):
            abuf[h2 * 2 + n // 2, :, (n % 2) * 256:(n % 2) * 256 + 256] = moved[h2 * 64:h2 * 64 + 64, :]

    place = pl.multiple_of(col * 64, 64)

    def piece(c):
        return tbuf.at[row, pl.ds(pl.multiple_of(c * 64, 64), 64)]

    for i, d in enumerate(a2a):
        push(abuf.at[peer(d)], piece(col), a_rs.at[i], (row, peer(d)))
    tbuf[row, pl.ds(place, 64), :] = abuf[col]

    w_up(0, 0, 1)
    w_dn(0, 0, 0)

    h2 = col // 2
    jj = lax.broadcasted_iota(jnp.int32, (OCC, BLOCK), 1)
    ii = lax.broadcasted_iota(jnp.int32, (OCC, BLOCK), 0)
    c_occ = jnp.zeros((OCC, BLOCK), jnp.float32)
    r_occ = jnp.zeros((OCC, BLOCK), jnp.float32)
    for p in range(OCC):
        c_occ = jnp.where(jj % OCC == p, eocc[h2, p], c_occ)
        r_occ = jnp.where(ii == p, eocc[row, p], r_occ)
    c_vir = jnp.zeros((OCC, BLOCK), jnp.float32)
    for q in range(32):
        c_vir = jnp.where(jj // OCC == q, evirt[h2 ^ g, core * 32 + q], c_vir)
    c_e = c_occ - c_vir
    ok = (jj % OCC < nocc[h2]) & (core * 32 + jj // OCC < nvirt[h2 ^ g]) & (ii < nocc[row])
    n_row = nvirt[row ^ g]

    def factor(q, _):
        e = (r_occ - evirt[row ^ g, q]) + c_e
        inv[pl.ds(pl.multiple_of(q * OCC, OCC), OCC), :] = jnp.where(ok & (q < n_row), 1.0 / e, 0.0)
        return 0

    lax.fori_loop(0, VIR, factor, 0)

    for half in range(2):
        for i, d in enumerate(a2a):
            if d[0] == half:
                c_from = col_of((xh + d[0]) % 2, (y + 4 - d[1]) % 4, (core + d[2]) % 2)
                arrived(piece(c_from), a_rs.at[i])
        t_up(0, 0, half)
        t_dn(0, 0, half)
        t_near(0, 0, half)

    w_in(0, 3, 0)
    w_up(0, 3, 0)
    w_in(0, 1, 1)
    w_dn(0, 1, 1)
    for j in range(2):
        w_in(1, 0, j)
        w_up(1, 0, j)
        w_dn(1, 0, j)
    t_in(0, 3, 0)
    t_up(0, 3, 0)
    t_in(0, 1, 1)
    t_dn(0, 1, 1)
    for j in range(2):
        t_in(1, 0, j)
        t_up(1, 0, j)
        t_dn(1, 0, j)
    w_in(0, 3, 1)
    w_in(0, 1, 0)
    t_in(0, 3, 1)
    t_in(0, 1, 0)
    w_in(0, 2, 0)
    w_in(0, 2, 1)
    for j in range(2):
        t_in(0, 2, j)
        t_near(0, 2, j)
    w_in(1, 3, 0)
    w_up(1, 3, 0)
    w_in(1, 1, 1)
    w_dn(1, 1, 1)
    w_in(1, 3, 1)
    w_in(1, 1, 0)
    for j in range(2):
        t_in(1, 3, j)
        t_in(1, 1, j)
    for j in range(2):
        w_in(1, 2, j)
        t_in(1, 2, j)
    for da in range(2):
        for db in range(4):
            for j in range(2):
                arrived(wslot(da, db, j, 1 - core), s_rs.at[da, db, j])

    out_ref[...] = jnp.zeros_like(out_ref)

    def product(i, _):
        h, m = i // 4, i % 4
        rows = pl.ds(pl.multiple_of(m * 256, 256), 256)
        part = jnp.dot(wbuf[h, 0, rows, :], tbuf[h, 0:512, :], preferred_element_type=jnp.float32)
        part += jnp.dot(wbuf[h, 1, rows, :], tbuf[h, 512:1024, :], preferred_element_type=jnp.float32)
        out_ref[rows, :] += part
        return 0

    lax.fori_loop(0, 32, product, 0)
    out_ref[...] = out_ref[...] * inv[...]
    for cp in sends:
        cp.wait_send()


def per_device(t2_pairs, cycle_ints, eps_occ, eps_virt, occ_count, virt_count, window_irrep):
    amps = t2_pairs.reshape(NIRREP, OCC, OCC * t2_pairs.shape[4], VIR)
    vmem = pl.BlockSpec(memory_space=pltpu.VMEM)
    smem = pl.BlockSpec(memory_space=pltpu.SMEM)
    return pl.pallas_call(
        kernel,
        out_shape=jax.ShapeDtypeStruct((ROWS, BLOCK), jnp.float32),
        in_specs=[vmem, pl.BlockSpec(memory_space=pl.ANY), smem, smem, smem, smem, smem],
        out_specs=vmem,
        scratch_shapes=[
            pltpu.VMEM((NIRREP, 2, ROWS, BLOCK), jnp.bfloat16),
            pltpu.VMEM((NIRREP, ROWS, BLOCK), jnp.bfloat16),
            pltpu.VMEM((16, 64, BLOCK), jnp.bfloat16),
            pltpu.VMEM((1024, 128), jnp.float32),
            pltpu.VMEM((512, 1024), jnp.bfloat16),
            pltpu.VMEM((ROWS, BLOCK), jnp.float32),
            pltpu.SemaphoreType.DMA((2, 4, 2)),
            pltpu.SemaphoreType.DMA((2, 4, 2)),
            pltpu.SemaphoreType.DMA((2, 4, 2)),
            pltpu.SemaphoreType.DMA((15,)),
            pltpu.SemaphoreType.DMA((N_SENDS,)),
            pltpu.SemaphoreType.DMA,
        ],
        compiler_params=pltpu.CompilerParams(
            collective_id=0, has_side_effects=True, vmem_limit_bytes=52 << 20),
    )(amps, cycle_ints, eps_occ, eps_virt, occ_count, virt_count, window_irrep)


def solution(mesh):
    placed = (P("row", None, None, None, "col", None), P("row", "col"), P(), P(), P(), P(), P())
    return jax.shard_map(
        per_device, mesh=mesh, in_specs=placed, out_specs=P("row", "col"), check_vma=False
    )
```

```python
import jax
import jax.numpy as jnp
from jax import lax
from jax.experimental import pallas as pl
from jax.experimental.pallas import tpu as pltpu
from jax.sharding import PartitionSpec as P

MESH = pl.DeviceIdType.MESH
NIRREP = 8
OCC = 16
VIR = 64
BLOCK = 512
ROWS = 1024
PART = 256
TILE = 512
N_SENDS = 110
DEPTH = 2
FIRST = [("w_up", 0, 0, 0), ("w_dn", 0, 0, 2), ("w_far", 0, 0, 0)]
ORDER = [
    ("w_up", 0, 0, 0), ("w_dn", 0, 0, 2), ("w_far", 0, 0, 0), ("w_up", 0, 0, 1), ("w_dn", 0, 0, 3),
    ("w_in", 0, 3, 0), ("w_in", 0, 1, 2), ("w_in", 1, 0, 0), ("t_in", 0, 0, 0), ("t_up", 0, 0, 0),
    ("t_dn", 0, 0, 0), ("t_near", 0, 0, 0), ("t_in", 0, 0, 1), ("t_up", 0, 0, 1),
    ("t_dn", 0, 0, 1), ("t_in", 0, 0, 2), ("t_up", 0, 0, 2), ("t_dn", 0, 0, 2), ("t_in", 0, 3, 0),
    ("t_in", 0, 1, 0), ("w_up", 0, 0, 2), ("w_dn", 0, 0, 0), ("w_far", 0, 0, 2), ("t_in", 0, 0, 3),
    ("t_up", 0, 0, 3), ("t_dn", 0, 0, 3), ("t_in", 0, 3, 1), ("t_in", 0, 1, 1), ("w_up", 0, 0, 3),
    ("w_dn", 0, 0, 1), ("t_near", 0, 0, 1), ("w_in", 0, 3, 1), ("w_in", 0, 1, 3),
    ("t_in", 1, 0, 0), ("t_up", 0, 3, 0), ("t_in", 0, 3, 2), ("t_in", 0, 1, 2), ("t_dn", 0, 1, 2),
    ("w_up", 0, 3, 0), ("w_dn", 0, 1, 2), ("w_far", 0, 0, 1), ("w_in", 0, 3, 2), ("w_in", 0, 1, 0),
    ("w_in", 1, 0, 2), ("t_up", 0, 3, 1), ("t_in", 0, 3, 3), ("t_in", 0, 1, 3), ("t_dn", 0, 1, 3),
    ("w_up", 0, 3, 1), ("w_dn", 0, 1, 3), ("t_near", 0, 0, 2), ("w_in", 0, 3, 3),
    ("w_in", 0, 1, 1), ("t_in", 1, 0, 1), ("prod", 0), ("t_up", 1, 0, 0), ("t_dn", 1, 0, 0),
    ("t_in", 0, 2, 0), ("t_in", 0, 2, 2), ("w_up", 1, 0, 0), ("w_dn", 1, 0, 2), ("w_far", 0, 0, 3),
    ("w_in", 0, 2, 0), ("w_in", 0, 2, 2), ("w_in", 1, 0, 1), ("t_up", 1, 0, 1), ("t_dn", 1, 0, 1),
    ("t_in", 0, 2, 1), ("t_in", 0, 2, 3), ("w_up", 1, 0, 2), ("w_dn", 1, 0, 0),
    ("t_near", 0, 0, 3), ("w_in", 0, 2, 1), ("w_in", 0, 2, 3), ("t_in", 1, 0, 2), ("prod", 1),
    ("t_up", 1, 0, 2), ("t_dn", 1, 0, 2), ("t_in", 1, 3, 0), ("t_in", 1, 1, 0), ("w_up", 1, 0, 1),
    ("t_near", 0, 2, 1), ("w_in", 1, 3, 0), ("w_in", 1, 1, 2), ("w_in", 1, 0, 3),
    ("w_dn", 1, 0, 3), ("t_in", 1, 3, 1), ("t_in", 1, 1, 1), ("w_up", 1, 0, 3), ("w_dn", 1, 0, 1),
    ("t_near", 0, 2, 2), ("w_in", 1, 3, 2), ("w_in", 1, 1, 0), ("t_in", 1, 0, 3),
    ("t_up", 1, 0, 3), ("t_dn", 1, 0, 3), ("prod", 2), ("t_up", 1, 3, 0), ("t_in", 1, 3, 2),
    ("t_in", 1, 1, 2), ("w_up", 1, 3, 0), ("w_dn", 1, 1, 2), ("w_far", 0, 2, 1), ("w_in", 1, 3, 1),
    ("w_in", 1, 1, 3), ("t_in", 1, 2, 1), ("t_in", 1, 3, 3), ("t_in", 1, 1, 3), ("t_dn", 1, 1, 3),
    ("w_dn", 1, 1, 3), ("w_in", 1, 3, 3), ("w_in", 1, 1, 1), ("t_in", 1, 2, 2), ("prod", 3),
    ("t_in", 1, 2, 0), ("t_in", 1, 2, 3), ("prod", 4), ("w_in", 1, 2, 0), ("w_in", 1, 2, 2),
    ("w_in", 1, 2, 1), ("w_in", 1, 2, 3),
]


def kernel(x_ref, w_ref, eocc, evirt, nocc, nvirt, window, out_ref, xbuf, wbuf, tbuf, abuf, s32, lhs,
           inv, acc, w_rs, s_rs, t_rs, a_rs, ss, loc, out_sem):
    row = lax.axis_index("row")
    col = lax.axis_index("col")
    z, xl = row // 2, row % 2
    xh, y, core = col // 8, (col // 2) % 4, col % 2
    sgn = 1 - 2 * core
    g = window[0]

    def col_of(a, b, k):
        return a * 8 + b * 2 + k

    y_up = (row, col_of(xh, (y + 4 + sgn) % 4, core))
    y_dn = (row, col_of(xh, (y + 4 - sgn) % 4, core))
    x_far = (row, col_of(1 - xh, y, core))
    sibling = (row, col_of(xh, y, 1 - core))
    z_up = (((z + 4 + sgn) % 4) * 2 + xl, col)
    z_dn = (((z + 4 - sgn) % 4) * 2 + xl, col)
    x_near = (z * 2 + 1 - xl, col)
    others = [(dx, dy, dk) for dx in range(2) for dy in (0, 1, 3, 2) for dk in range(2)
              if (dx, dy, dk) != (0, 0, 0)]

    def peer(d):
        return col_of((xh + d[0]) % 2, (y + d[1]) % 4, (core + d[2]) % 2)

    barrier = pltpu.get_barrier_semaphore()
    for d in others:
        pl.semaphore_signal(barrier, inc=1, device_id=(row, peer(d)), device_id_type=MESH)
    for dev in (z_up, z_dn, x_near):
        pl.semaphore_signal(barrier, inc=1, device_id=dev, device_id_type=MESH)

    amps = pltpu.make_async_copy(x_ref, xbuf, loc.at[0])
    amps.start()
    mine = pltpu.make_async_copy(w_ref, wbuf.at[xh * 4 + y, core], loc.at[1])
    mine.start()
    amps.wait()

    rid = lax.broadcasted_iota(jnp.int32, (64, 128), 0)
    lane = lax.broadcasted_iota(jnp.int32, (64, 128), 1)
    live_src = (rid % OCC < nocc[row]) & (col * 4 + rid // OCC < nvirt[row ^ g])

    def prepare(h2, _):
        for p in range(OCC):
            s32[pl.ds(p, 64, stride=OCC), 0:VIR] = xbuf[h2, p].astype(jnp.float32)
        for pair in range(8):
            lo = s32[pl.ds(pair * 128, 64), :]
            hi = pltpu.roll(s32[pl.ds(pair * 128 + 64, 64), :], 64, 1)
            both = jnp.where(live_src, jnp.where(lane < VIR, lo, hi), 0.0)
            lhs[pl.ds(h2 * 64, 64), pl.ds(pair * 128, 128)] = both.astype(jnp.bfloat16)
        return 0

    lax.fori_loop(0, NIRREP, prepare, 0)
    mine.wait()
    pl.semaphore_wait(barrier, len(others) + 3)

    sends = []
    waiting = []
    in_flight = {}

    def push(src, dst, rsem, dev, way=None):
        queue = in_flight.setdefault(way, [])
        if way is not None and len(queue) == DEPTH:
            queue.pop(0).wait_send()
        cp = pltpu.make_async_remote_copy(
            src_ref=src, dst_ref=dst, send_sem=ss.at[len(sends)], recv_sem=rsem,
            device_id=dev, device_id_type=MESH)
        cp.start()
        sends.append(cp)
        queue.append(cp)

    def arrived(ref, rsem):
        pltpu.make_async_remote_copy(
            src_ref=ref, dst_ref=ref, send_sem=ss.at[N_SENDS - 1], recv_sem=rsem,
            device_id=sibling, device_id_type=MESH).wait_recv()

    def wslot(da, db, j):
        return wbuf.at[((xh + da) % 2) * 4 + (y + 4 + sgn * db) % 4, core, pl.ds(j * PART, PART)]

    def trows(j):
        return pl.multiple_of(((xh + j // 2) % 2) * 512 + ((y // 2 + j % 2) % 2) * 256, 256)

    def tslot(da, db, j):
        return tbuf.at[((z + 4 + sgn * db) % 4) * 2 + (xl + da) % 2, pl.ds(trows(j), PART)]

    def send(op, da, db, j):
        slot, sems = (wslot, w_rs) if op[0] == "w" else (tslot, t_rs)
        dev, da2, db2 = {
            "w_up": (y_up, da, db + 3), "w_dn": (y_dn, da, db + 1), "w_far": (x_far, 1 - da, db),
            "t_up": (z_up, da, db + 3), "t_dn": (z_dn, da, db + 1), "t_near": (x_near, 1 - da, db),
        }[op]
        ref = slot(da, db, j)
        way = "x" if op in ("w_far", "t_near") else op
        push(ref, ref, sems.at[da2, db2 % 4, j], dev, way)

    def share(da, db, j):
        ref = wslot(da, db, j)
        push(ref, ref, s_rs.at[da, db, j], sibling)
        waiting.append((da, db, j))

    def w_in(da, db, j):
        arrived(wslot(da, db, j), w_rs.at[da, db, j])
        share(da, db, j)

    def t_in(da, db, j):
        if (da, db) != (0, 0):
            arrived(tslot(da, db, j), t_rs.at[da, db, j])
            return
        a = (xh + j // 2) % 2
        for i in range(2):
            for k in range(2):
                b = ((y // 2 + j % 2) % 2) * 2 + (y + i) % 2
                if (j, i, k) != (0, 0, 0):
                    c = col_of(a, b, (core + k) % 2)
                    arrived(piece(c), a_rs.at[c])

    def shared(da, db, j):
        ref = wbuf.at[((xh + da) % 2) * 4 + (y + 4 - sgn * db) % 4, 1 - core, pl.ds(j * PART, PART)]
        arrived(ref, s_rs.at[da, db, j])

    def piece(c):
        return tbuf.at[row, pl.ds(pl.multiple_of(c * 64, 64), 64)]

    for op in FIRST:
        send(*op)
    for j in range(4):
        share(0, 0, j)

    src = lax.broadcasted_iota(jnp.int32, (1024, 256), 0)
    dst = lax.broadcasted_iota(jnp.int32, (1024, 256), 1)
    code = (src % VIR) * OCC + src // VIR
    for n in range(4):
        onehot = jnp.where(code == dst + n * 256, 1.0, 0.0).astype(jnp.bfloat16)
        moved = jnp.dot(lhs[...], onehot, preferred_element_type=jnp.float32).astype(jnp.bfloat16)
        for h2 in range(NIRREP):
            abuf[h2 * 2 + n // 2, :, (n % 2) * 256:(n % 2) * 256 + 256] = moved[h2 * 64:h2 * 64 + 64, :]

    for d in others:
        push(abuf.at[peer(d)], piece(col), a_rs.at[col], (row, peer(d)))
    tbuf[row, pl.ds(pl.multiple_of(col * 64, 64), 64), :] = abuf[col]

    h2 = col // 2
    jj = lax.broadcasted_iota(jnp.int32, (OCC, BLOCK), 1)
    ii = lax.broadcasted_iota(jnp.int32, (OCC, BLOCK), 0)
    c_occ = jnp.zeros((OCC, BLOCK), jnp.float32)
    r_occ = jnp.zeros((OCC, BLOCK), jnp.float32)
    for p in range(OCC):
        c_occ = jnp.where(jj % OCC == p, eocc[h2, p], c_occ)
        r_occ = jnp.where(ii == p, eocc[row, p], r_occ)
    c_vir = jnp.zeros((OCC, BLOCK), jnp.float32)
    for q in range(32):
        c_vir = jnp.where(jj // OCC == q, evirt[h2 ^ g, core * 32 + q], c_vir)
    c_e = c_occ - c_vir
    ok = (jj % OCC < nocc[h2]) & (core * 32 + jj // OCC < nvirt[h2 ^ g]) & (ii < nocc[row])
    n_row = nvirt[row ^ g]

    def factor(q, _):
        e = (r_occ - evirt[row ^ g, q]) + c_e
        inv[pl.ds(pl.multiple_of(q * OCC, OCC), OCC), :] = jnp.where(ok & (q < n_row), 1.0 / e, 0.0)
        return 0

    lax.fori_loop(0, VIR, factor, 0)
    acc[...] = jnp.zeros_like(acc)

    def part(h, rows):
        return (jnp.dot(wbuf[h, 0, rows, :], tbuf[h, 0:512, :], preferred_element_type=jnp.float32)
                + jnp.dot(wbuf[h, 1, rows, :], tbuf[h, 512:1024, :], preferred_element_type=jnp.float32))

    def product(h):
        def step(m, _):
            rows = pl.ds(pl.multiple_of(m * TILE, TILE), TILE)
            acc[rows, :] += part(h, rows)
            return 0
        lax.fori_loop(0, ROWS // TILE, step, 0)

    def rank(da, db):
        dist = (db * (4 - db) + 2) // 3
        return da * (2 + dist) + (1 - da) * (dist // 2)

    def stage_of(da, db):
        d = min(db, 4 - db)
        return 2 + d if da else d // 2

    def products(stage):
        for key in [k for k in waiting if stage_of(*k[:2]) <= stage and stage < 4]:
            waiting.remove(key)
            shared(*key)

        def each(h, _):
            by_w = rank((h // 4 + xh) % 2, (h % 4 + 4 - y) % 4)
            by_t = rank((h % 2 + xl) % 2, (h // 2 + 4 - z) % 4)

            @pl.when((by_w <= stage) & (by_t <= stage) & ((by_w == stage) | (by_t == stage)) & (by_w < 4))
            def _():
                product(h)
            return 0

        lax.fori_loop(0, NIRREP, each, 0)

    for op in ORDER:
        if op in FIRST:
            continue
        if op[0] == "prod":
            products(op[1])
        elif op[0] == "w_in":
            w_in(*op[1:])
        elif op[0] == "t_in":
            t_in(*op[1:])
        else:
            send(*op)

    last = (1 - xh) * 4 + (y + 2) % 4
    copies = []
    for key in waiting:
        shared(*key)
    for m in range(ROWS // PART):
        rows = pl.ds(m * PART, PART)
        acc[rows, :] = (acc[rows, :] + part(last, rows)) * inv[rows, :]
        cp = pltpu.make_async_copy(acc.at[rows], out_ref.at[rows], out_sem.at[m])
        cp.start()
        copies.append(cp)
    for queue in in_flight.values():
        for cp in queue:
            cp.wait_send()
    for cp in copies:
        cp.wait()


def per_device(t2_pairs, cycle_ints, eps_occ, eps_virt, occ_count, virt_count, window_irrep):
    amps = t2_pairs.reshape(NIRREP, OCC, OCC * t2_pairs.shape[4], VIR)
    hbm = pl.BlockSpec(memory_space=pl.ANY)
    smem = pl.BlockSpec(memory_space=pltpu.SMEM)
    return pl.pallas_call(
        kernel,
        out_shape=jax.ShapeDtypeStruct((ROWS, BLOCK), jnp.float32),
        in_specs=[hbm, hbm, smem, smem, smem, smem, smem],
        out_specs=hbm,
        scratch_shapes=[
            pltpu.VMEM((NIRREP, OCC, 64, VIR), jnp.bfloat16),
            pltpu.VMEM((NIRREP, 2, ROWS, BLOCK), jnp.bfloat16),
            pltpu.VMEM((NIRREP, ROWS, BLOCK), jnp.bfloat16),
            pltpu.VMEM((16, 64, BLOCK), jnp.bfloat16),
            pltpu.VMEM((1024, 128), jnp.float32),
            pltpu.VMEM((512, 1024), jnp.bfloat16),
            pltpu.VMEM((ROWS, BLOCK), jnp.float32),
            pltpu.VMEM((ROWS, BLOCK), jnp.float32),
            pltpu.SemaphoreType.DMA((2, 4, 4)),
            pltpu.SemaphoreType.DMA((2, 4, 4)),
            pltpu.SemaphoreType.DMA((2, 4, 4)),
            pltpu.SemaphoreType.DMA((16,)),
            pltpu.SemaphoreType.DMA((N_SENDS,)),
            pltpu.SemaphoreType.DMA((2,)),
            pltpu.SemaphoreType.DMA((ROWS // PART,)),
        ],
        compiler_params=pltpu.CompilerParams(
            collective_id=0, has_side_effects=True, vmem_limit_bytes=63 << 20),
    )(amps, cycle_ints, eps_occ, eps_virt, occ_count, virt_count, window_irrep)


def solution(mesh):
    placed = (P("row", None, None, None, "col", None), P("row", "col"), P(), P(), P(), P(), P())
    return jax.shard_map(
        per_device, mesh=mesh, in_specs=placed, out_specs=P("row", "col"), check_vma=False
    )
```

```python
import jax
import jax.numpy as jnp
from jax import lax
from jax.experimental import pallas as pl
from jax.experimental.pallas import tpu as pltpu
from jax.sharding import PartitionSpec as P

MESH = pl.DeviceIdType.MESH
NIRREP = 8
OCC = 16
VIR = 64
BLOCK = 512
ROWS = 1024
PART = 256
TILE = 512
N_SENDS = 110
DEPTH = 3
FIRST = [("w_up", 0, 0, 0), ("w_dn", 0, 0, 2), ("w_far", 0, 0, 0)]
ORDER = [
    ("w_up", 0, 0, 0), ("w_dn", 0, 0, 2), ("w_far", 0, 0, 0), ("w_up", 0, 0, 1), ("w_dn", 0, 0, 3),
    ("w_in", 0, 3, 0), ("w_in", 0, 1, 2), ("w_in", 1, 0, 0), ("t_in", 0, 0, 0), ("t_up", 0, 0, 0),
    ("t_dn", 0, 0, 0), ("t_near", 0, 0, 0), ("t_in", 0, 0, 1), ("t_up", 0, 0, 1),
    ("t_dn", 0, 0, 1), ("w_up", 0, 0, 2), ("w_dn", 0, 0, 0), ("w_far", 0, 0, 2), ("t_in", 0, 0, 2),
    ("t_up", 0, 0, 2), ("t_dn", 0, 0, 2), ("t_in", 0, 3, 0), ("t_in", 0, 1, 0), ("t_in", 0, 0, 3),
    ("t_up", 0, 0, 3), ("t_dn", 0, 0, 3), ("w_up", 0, 0, 3), ("w_dn", 0, 0, 1),
    ("t_near", 0, 0, 1), ("t_in", 0, 3, 1), ("t_in", 0, 1, 1), ("w_in", 0, 3, 1),
    ("w_in", 0, 1, 3), ("t_in", 1, 0, 0), ("t_up", 0, 3, 0), ("w_up", 0, 3, 0), ("w_dn", 0, 1, 2),
    ("w_far", 0, 0, 1), ("t_in", 0, 3, 2), ("t_in", 0, 1, 2), ("t_dn", 0, 1, 2), ("w_in", 0, 3, 2),
    ("w_in", 0, 1, 0), ("w_in", 1, 0, 2), ("t_up", 0, 3, 1), ("w_up", 0, 3, 1), ("w_dn", 0, 1, 3),
    ("t_near", 0, 0, 2), ("t_in", 0, 3, 3), ("t_in", 0, 1, 3), ("t_dn", 0, 1, 3),
    ("w_in", 0, 3, 3), ("w_in", 0, 1, 1), ("t_in", 1, 0, 1), ("t_up", 1, 0, 0), ("t_dn", 1, 0, 0),
    ("w_up", 1, 0, 0), ("w_dn", 1, 0, 2), ("w_far", 0, 0, 3), ("prod", 0, 0), ("t_in", 0, 2, 0),
    ("t_in", 0, 2, 2), ("w_in", 0, 2, 0), ("w_in", 0, 2, 2), ("w_in", 1, 0, 1), ("prod", 0, 1),
    ("t_up", 1, 0, 1), ("t_dn", 1, 0, 1), ("w_up", 1, 0, 2), ("w_dn", 1, 0, 0),
    ("t_near", 0, 0, 3), ("t_in", 0, 2, 1), ("t_in", 0, 2, 3), ("w_in", 0, 2, 1),
    ("w_in", 0, 2, 3), ("t_in", 1, 0, 2), ("t_up", 1, 0, 2), ("t_dn", 1, 0, 2), ("w_up", 1, 0, 1),
    ("t_near", 0, 2, 1), ("prod", 1, 0), ("t_in", 1, 3, 0), ("t_in", 1, 1, 0), ("w_in", 1, 3, 0),
    ("w_in", 1, 1, 2), ("w_in", 1, 0, 3), ("w_dn", 1, 0, 3), ("prod", 1, 1), ("w_up", 1, 0, 3),
    ("w_dn", 1, 0, 1), ("w_far", 0, 2, 1), ("t_in", 1, 3, 1), ("t_in", 1, 1, 1), ("w_in", 1, 3, 2),
    ("w_in", 1, 1, 0), ("t_in", 1, 0, 3), ("t_up", 1, 0, 3), ("t_dn", 1, 0, 3), ("t_up", 1, 3, 0),
    ("w_up", 1, 3, 0), ("w_far", 0, 2, 2), ("prod", 2, 0), ("t_in", 1, 3, 2), ("t_in", 1, 1, 2),
    ("t_dn", 1, 1, 2), ("w_in", 1, 3, 1), ("w_in", 1, 1, 3), ("t_in", 1, 2, 1), ("w_dn", 1, 1, 3),
    ("prod", 2, 1), ("t_in", 1, 3, 3), ("t_in", 1, 1, 3), ("t_dn", 1, 1, 3), ("w_in", 1, 3, 3),
    ("w_in", 1, 1, 1), ("w_in", 1, 2, 1), ("prod", 3, 0), ("t_in", 1, 2, 0), ("t_in", 1, 2, 2),
    ("w_in", 1, 2, 0), ("w_in", 1, 2, 3), ("w_in", 1, 2, 2), ("prod", 3, 1), ("t_in", 1, 2, 3),
]


def kernel(x_ref, w_ref, eocc, evirt, nocc, nvirt, window, out_ref, xbuf, wbuf, tbuf, abuf, s32, lhs,
           inv, acc, w_rs, s_rs, t_rs, a_rs, ss, loc, out_sem):
    row = lax.axis_index("row")
    col = lax.axis_index("col")
    z, xl = row // 2, row % 2
    xh, y, core = col // 8, (col // 2) % 4, col % 2
    sgn = 1 - 2 * core
    g = window[0]

    def col_of(a, b, k):
        return a * 8 + b * 2 + k

    y_up = (row, col_of(xh, (y + 4 + sgn) % 4, core))
    y_dn = (row, col_of(xh, (y + 4 - sgn) % 4, core))
    x_far = (row, col_of(1 - xh, y, core))
    sibling = (row, col_of(xh, y, 1 - core))
    z_up = (((z + 4 + sgn) % 4) * 2 + xl, col)
    z_dn = (((z + 4 - sgn) % 4) * 2 + xl, col)
    x_near = (z * 2 + 1 - xl, col)
    others = [(dx, dy, dk) for dx in range(2) for dy in (0, 1, 3, 2) for dk in range(2)
              if (dx, dy, dk) != (0, 0, 0)]

    def peer(d):
        return col_of((xh + d[0]) % 2, (y + d[1]) % 4, (core + d[2]) % 2)

    barrier = pltpu.get_barrier_semaphore()
    for d in others:
        pl.semaphore_signal(barrier, inc=1, device_id=(row, peer(d)), device_id_type=MESH)
    for dev in (z_up, z_dn, x_near):
        pl.semaphore_signal(barrier, inc=1, device_id=dev, device_id_type=MESH)

    amps = pltpu.make_async_copy(x_ref, xbuf, loc.at[0])
    amps.start()
    mine = pltpu.make_async_copy(w_ref, wbuf.at[xh * 4 + y, core], loc.at[1])
    mine.start()

    sends = []
    waiting = []
    in_flight = {}

    def push(src, dst, rsem, dev, way=None):
        queue = in_flight.setdefault(way, [])
        if way is not None and len(queue) == DEPTH:
            queue.pop(0).wait_send()
        cp = pltpu.make_async_remote_copy(
            src_ref=src, dst_ref=dst, send_sem=ss.at[len(sends)], recv_sem=rsem,
            device_id=dev, device_id_type=MESH)
        cp.start()
        sends.append(cp)
        queue.append(cp)

    def arrived(ref, rsem):
        pltpu.make_async_remote_copy(
            src_ref=ref, dst_ref=ref, send_sem=ss.at[N_SENDS - 1], recv_sem=rsem,
            device_id=sibling, device_id_type=MESH).wait_recv()

    def wslot(da, db, j):
        return wbuf.at[((xh + da) % 2) * 4 + (y + 4 + sgn * db) % 4, core, pl.ds(j * PART, PART)]

    def trows(j):
        return pl.multiple_of(((xh + j // 2) % 2) * 512 + ((y // 2 + j % 2) % 2) * 256, 256)

    def tslot(da, db, j):
        return tbuf.at[((z + 4 + sgn * db) % 4) * 2 + (xl + da) % 2, pl.ds(trows(j), PART)]

    def send(op, da, db, j):
        slot, sems = (wslot, w_rs) if op[0] == "w" else (tslot, t_rs)
        dev, da2, db2 = {
            "w_up": (y_up, da, db + 3), "w_dn": (y_dn, da, db + 1), "w_far": (x_far, 1 - da, db),
            "t_up": (z_up, da, db + 3), "t_dn": (z_dn, da, db + 1), "t_near": (x_near, 1 - da, db),
        }[op]
        ref = slot(da, db, j)
        way = "x" if op in ("w_far", "t_near") else op
        push(ref, ref, sems.at[da2, db2 % 4, j], dev, way)

    def share(da, db, j):
        ref = wslot(da, db, j)
        push(ref, ref, s_rs.at[da, db, j], sibling)
        waiting.append((da, db, j))

    def w_in(da, db, j):
        arrived(wslot(da, db, j), w_rs.at[da, db, j])
        share(da, db, j)

    def t_in(da, db, j):
        if (da, db) != (0, 0):
            arrived(tslot(da, db, j), t_rs.at[da, db, j])
            return
        a = (xh + j // 2) % 2
        for i in range(2):
            for k in range(2):
                b = ((y // 2 + j % 2) % 2) * 2 + (y + i) % 2
                if (j, i, k) != (0, 0, 0):
                    c = col_of(a, b, (core + k) % 2)
                    arrived(piece(c), a_rs.at[c])

    def shared(da, db, j):
        ref = wbuf.at[((xh + da) % 2) * 4 + (y + 4 - sgn * db) % 4, 1 - core, pl.ds(j * PART, PART)]
        arrived(ref, s_rs.at[da, db, j])

    def piece(c):
        return tbuf.at[row, pl.ds(pl.multiple_of(c * 64, 64), 64)]

    amps.wait()

    rid = lax.broadcasted_iota(jnp.int32, (64, 128), 0)
    lane = lax.broadcasted_iota(jnp.int32, (64, 128), 1)
    live_src = (rid % OCC < nocc[row]) & (col * 4 + rid // OCC < nvirt[row ^ g])

    def prepare(h2, _):
        for p in range(OCC):
            s32[pl.ds(p, 64, stride=OCC), 0:VIR] = xbuf[h2, p].astype(jnp.float32)
        for pair in range(8):
            lo = s32[pl.ds(pair * 128, 64), :]
            hi = pltpu.roll(s32[pl.ds(pair * 128 + 64, 64), :], 64, 1)
            both = jnp.where(live_src, jnp.where(lane < VIR, lo, hi), 0.0)
            lhs[pl.ds(h2 * 64, 64), pl.ds(pair * 128, 128)] = both.astype(jnp.bfloat16)
        return 0

    lax.fori_loop(0, NIRREP, prepare, 0)
    mine.wait()
    pl.semaphore_wait(barrier, len(others) + 3)
    for op in FIRST:
        send(*op)
    for j in range(4):
        share(0, 0, j)

    src = lax.broadcasted_iota(jnp.int32, (1024, 256), 0)
    dst = lax.broadcasted_iota(jnp.int32, (1024, 256), 1)
    code = (src % VIR) * OCC + src // VIR
    for n in range(4):
        onehot = jnp.where(code == dst + n * 256, 1.0, 0.0).astype(jnp.bfloat16)
        moved = jnp.dot(lhs[...], onehot, preferred_element_type=jnp.float32).astype(jnp.bfloat16)
        for h2 in range(NIRREP):
            abuf[h2 * 2 + n // 2, :, (n % 2) * 256:(n % 2) * 256 + 256] = moved[h2 * 64:h2 * 64 + 64, :]

    for d in others:
        push(abuf.at[peer(d)], piece(col), a_rs.at[col], (row, peer(d)))
    tbuf[row, pl.ds(pl.multiple_of(col * 64, 64), 64), :] = abuf[col]

    h2 = col // 2
    jj = lax.broadcasted_iota(jnp.int32, (OCC, BLOCK), 1)
    ii = lax.broadcasted_iota(jnp.int32, (OCC, BLOCK), 0)
    c_occ = jnp.zeros((OCC, BLOCK), jnp.float32)
    r_occ = jnp.zeros((OCC, BLOCK), jnp.float32)
    for p in range(OCC):
        c_occ = jnp.where(jj % OCC == p, eocc[h2, p], c_occ)
        r_occ = jnp.where(ii == p, eocc[row, p], r_occ)
    c_vir = jnp.zeros((OCC, BLOCK), jnp.float32)
    for q in range(32):
        c_vir = jnp.where(jj // OCC == q, evirt[h2 ^ g, core * 32 + q], c_vir)
    c_e = c_occ - c_vir
    ok = (jj % OCC < nocc[h2]) & (core * 32 + jj // OCC < nvirt[h2 ^ g]) & (ii < nocc[row])
    n_row = nvirt[row ^ g]

    def factor(q, _):
        e = (r_occ - evirt[row ^ g, q]) + c_e
        inv[pl.ds(pl.multiple_of(q * OCC, OCC), OCC), :] = jnp.where(ok & (q < n_row), 1.0 / e, 0.0)
        return 0

    lax.fori_loop(0, VIR, factor, 0)
    acc[...] = jnp.zeros_like(acc)

    def part(h, rows):
        return (jnp.dot(wbuf[h, 0, rows, :], tbuf[h, 0:512, :], preferred_element_type=jnp.float32)
                + jnp.dot(wbuf[h, 1, rows, :], tbuf[h, 512:1024, :], preferred_element_type=jnp.float32))

    def product(h, m):
        rows = pl.ds(m * TILE, TILE)
        acc[rows, :] += part(h, rows)

    def rank(da, db):
        dist = (db * (4 - db) + 2) // 3
        return da * (2 + dist) + (1 - da) * (dist // 2)

    def stage_of(da, db):
        d = min(db, 4 - db)
        return 2 + d if da else d // 2

    last_w = (1 - xh) * 4 + (y + 2) % 4
    last_t = ((z + 2) % 4) * 2 + 1 - xl

    def products(stage, m):
        for key in [k for k in waiting if stage_of(*k[:2]) <= stage]:
            waiting.remove(key)
            shared(*key)

        def each(h, _):
            by_w = rank((h // 4 + xh) % 2, (h % 4 + 4 - y) % 4)
            by_t = rank((h % 2 + xl) % 2, (h // 2 + 4 - z) % 4)

            @pl.when((by_w <= stage) & (by_t <= stage) & ((by_w == stage) | (by_t == stage)))
            def _():
                product(h, m)
            return 0

        lax.fori_loop(0, NIRREP, each, 0)

    def quarter(j):

        @pl.when(last_w != last_t)
        def _():
            cols = pl.ds(pl.multiple_of(((y // 2 + j % 2) % 2) * 256, 256), 256)
            for m in range(ROWS // TILE):
                rows = pl.ds(m * TILE, TILE)
                acc[rows, :] += jnp.dot(wbuf[last_t, (xh + j // 2) % 2, rows, cols],
                                        tbuf[last_t, pl.ds(trows(j), PART), :],
                                        preferred_element_type=jnp.float32)

    copies = []

    def finish(da, db, j):
        waiting.remove((da, db, j))
        shared(da, db, j)
        rows = pl.ds(j * PART, PART)
        acc[rows, :] = (acc[rows, :] + part(last_w, rows)) * inv[rows, :]
        cp = pltpu.make_async_copy(acc.at[rows], out_ref.at[rows], out_sem.at[j])
        cp.start()
        copies.append(cp)

    final = [op for op in ORDER if op[0] == "w_in" and op[1:3] == (1, 2)]
    for op in ORDER:
        if op in FIRST:
            continue
        if op[0] == "prod":
            products(*op[1:])
        elif op[0] == "w_in":
            w_in(*op[1:])
        elif op[0] == "t_in":
            t_in(*op[1:])
        else:
            send(*op)
    for j in range(4):
        quarter(j)
    for i, op in enumerate(final):
        finish(*op[1:])
    for queue in in_flight.values():
        for cp in queue:
            cp.wait_send()
    for cp in copies:
        cp.wait()


def per_device(t2_pairs, cycle_ints, eps_occ, eps_virt, occ_count, virt_count, window_irrep):
    amps = t2_pairs.reshape(NIRREP, OCC, OCC * t2_pairs.shape[4], VIR)
    hbm = pl.BlockSpec(memory_space=pl.ANY)
    smem = pl.BlockSpec(memory_space=pltpu.SMEM)
    return pl.pallas_call(
        kernel,
        out_shape=jax.ShapeDtypeStruct((ROWS, BLOCK), jnp.float32),
        in_specs=[hbm, hbm, smem, smem, smem, smem, smem],
        out_specs=hbm,
        scratch_shapes=[
            pltpu.VMEM((NIRREP, OCC, 64, VIR), jnp.bfloat16),
            pltpu.VMEM((NIRREP, 2, ROWS, BLOCK), jnp.bfloat16),
            pltpu.VMEM((NIRREP, ROWS, BLOCK), jnp.bfloat16),
            pltpu.VMEM((16, 64, BLOCK), jnp.bfloat16),
            pltpu.VMEM((1024, 128), jnp.float32),
            pltpu.VMEM((512, 1024), jnp.bfloat16),
            pltpu.VMEM((ROWS, BLOCK), jnp.float32),
            pltpu.VMEM((ROWS, BLOCK), jnp.float32),
            pltpu.SemaphoreType.DMA((2, 4, 4)),
            pltpu.SemaphoreType.DMA((2, 4, 4)),
            pltpu.SemaphoreType.DMA((2, 4, 4)),
            pltpu.SemaphoreType.DMA((16,)),
            pltpu.SemaphoreType.DMA((N_SENDS,)),
            pltpu.SemaphoreType.DMA((2,)),
            pltpu.SemaphoreType.DMA((ROWS // PART,)),
        ],
        compiler_params=pltpu.CompilerParams(
            collective_id=0, has_side_effects=True, vmem_limit_bytes=63 << 20),
    )(amps, cycle_ints, eps_occ, eps_virt, occ_count, virt_count, window_irrep)


def solution(mesh):
    placed = (P("row", None, None, None, "col", None), P("row", "col"), P(), P(), P(), P(), P())
    return jax.shard_map(
        per_device, mesh=mesh, in_specs=placed, out_specs=P("row", "col"), check_vma=False
    )
```

```python
import jax
import jax.numpy as jnp
from jax import lax
from jax.experimental import pallas as pl
from jax.experimental.pallas import tpu as pltpu
from jax.sharding import PartitionSpec as P

MESH = pl.DeviceIdType.MESH
NIRREP = 8
OCC = 16
VIR = 64
BLOCK = 512
ROWS = 1024
PART = 256
TILE = 512
N_SENDS = 110
DEPTH = 3
FIRST = [("w_up", 0, 0, 0), ("w_dn", 0, 0, 2), ("w_far", 0, 0, 0)]
ORDER = [
    ("w_up", 0, 0, 0), ("w_dn", 0, 0, 2), ("w_far", 0, 0, 0), ("w_up", 0, 0, 1), ("w_dn", 0, 0, 3),
    ("w_in", 0, 3, 0), ("w_in", 0, 1, 2), ("w_in", 1, 0, 0), ("t_in", 0, 0, 0), ("t_up", 0, 0, 0),
    ("t_dn", 0, 0, 0), ("t_near", 0, 0, 0), ("t_in", 0, 0, 1), ("t_up", 0, 0, 1),
    ("t_dn", 0, 0, 1), ("w_up", 0, 0, 2), ("w_dn", 0, 0, 0), ("w_far", 0, 0, 2), ("t_in", 0, 0, 2),
    ("t_up", 0, 0, 2), ("t_dn", 0, 0, 2), ("t_in", 0, 3, 0), ("t_in", 0, 1, 0), ("t_in", 0, 0, 3),
    ("t_up", 0, 0, 3), ("t_dn", 0, 0, 3), ("w_up", 0, 0, 3), ("w_dn", 0, 0, 1),
    ("t_near", 0, 0, 1), ("t_in", 0, 3, 1), ("t_in", 0, 1, 1), ("w_in", 0, 3, 1),
    ("w_in", 0, 1, 3), ("t_in", 1, 0, 0), ("t_up", 0, 3, 0), ("w_up", 0, 3, 0), ("w_dn", 0, 1, 2),
    ("w_far", 0, 0, 1), ("t_in", 0, 3, 2), ("t_in", 0, 1, 2), ("t_dn", 0, 1, 2), ("w_in", 0, 3, 2),
    ("w_in", 0, 1, 0), ("w_in", 1, 0, 2), ("t_up", 0, 3, 1), ("w_up", 0, 3, 1), ("w_dn", 0, 1, 3),
    ("t_near", 0, 0, 2), ("t_in", 0, 3, 3), ("t_in", 0, 1, 3), ("t_dn", 0, 1, 3),
    ("w_in", 0, 3, 3), ("w_in", 0, 1, 1), ("t_in", 1, 0, 1), ("t_up", 1, 0, 0), ("t_dn", 1, 0, 0),
    ("w_up", 1, 0, 0), ("w_dn", 1, 0, 2), ("w_far", 0, 0, 3), ("prod", 0, 0), ("t_in", 0, 2, 0),
    ("t_in", 0, 2, 2), ("w_in", 0, 2, 0), ("w_in", 0, 2, 2), ("w_in", 1, 0, 1), ("prod", 0, 1),
    ("t_up", 1, 0, 1), ("t_dn", 1, 0, 1), ("w_up", 1, 0, 2), ("w_dn", 1, 0, 0),
    ("t_near", 0, 0, 3), ("t_in", 0, 2, 1), ("t_in", 0, 2, 3), ("w_in", 0, 2, 1),
    ("w_in", 0, 2, 3), ("t_in", 1, 0, 2), ("t_up", 1, 0, 2), ("t_dn", 1, 0, 2), ("w_up", 1, 0, 1),
    ("t_near", 0, 2, 1), ("prod", 1, 0), ("t_in", 1, 3, 0), ("t_in", 1, 1, 0), ("w_in", 1, 3, 0),
    ("w_in", 1, 1, 2), ("w_in", 1, 0, 3), ("w_dn", 1, 0, 3), ("prod", 1, 1), ("w_up", 1, 0, 3),
    ("w_dn", 1, 0, 1), ("w_far", 0, 2, 1), ("t_in", 1, 3, 1), ("t_in", 1, 1, 1), ("w_in", 1, 3, 2),
    ("w_in", 1, 1, 0), ("t_in", 1, 0, 3), ("t_up", 1, 0, 3), ("t_dn", 1, 0, 3), ("t_up", 1, 3, 0),
    ("w_up", 1, 3, 0), ("w_far", 0, 2, 2), ("prod", 2, 0), ("t_in", 1, 3, 2), ("t_in", 1, 1, 2),
    ("t_dn", 1, 1, 2), ("w_in", 1, 3, 1), ("w_in", 1, 1, 3), ("t_in", 1, 2, 1), ("w_dn", 1, 1, 3),
    ("prod", 2, 1), ("t_in", 1, 3, 3), ("t_in", 1, 1, 3), ("t_dn", 1, 1, 3), ("w_in", 1, 3, 3),
    ("w_in", 1, 1, 1), ("w_in", 1, 2, 1), ("prod", 3, 0), ("t_in", 1, 2, 0), ("t_in", 1, 2, 2),
    ("w_in", 1, 2, 0), ("w_in", 1, 2, 3), ("w_in", 1, 2, 2), ("prod", 3, 1), ("t_in", 1, 2, 3),
]


def kernel(x_ref, w_ref, eocc, evirt, nocc, nvirt, window, acc, xbuf, wbuf, tbuf, abuf, s32, lhs,
           inv, w_rs, s_rs, t_rs, a_rs, ss, loc):
    row = lax.axis_index("row")
    col = lax.axis_index("col")
    z, xl = row // 2, row % 2
    xh, y, core = col // 8, (col // 2) % 4, col % 2
    sgn = 1 - 2 * core
    g = window[0]

    def col_of(a, b, k):
        return a * 8 + b * 2 + k

    y_up = (row, col_of(xh, (y + 4 + sgn) % 4, core))
    y_dn = (row, col_of(xh, (y + 4 - sgn) % 4, core))
    x_far = (row, col_of(1 - xh, y, core))
    sibling = (row, col_of(xh, y, 1 - core))
    z_up = (((z + 4 + sgn) % 4) * 2 + xl, col)
    z_dn = (((z + 4 - sgn) % 4) * 2 + xl, col)
    x_near = (z * 2 + 1 - xl, col)
    others = [(dx, dy, dk) for dx in range(2) for dy in (0, 1, 3, 2) for dk in range(2)
              if (dx, dy, dk) != (0, 0, 0)]

    def peer(d):
        return col_of((xh + d[0]) % 2, (y + d[1]) % 4, (core + d[2]) % 2)

    barrier = pltpu.get_barrier_semaphore()
    for d in others:
        pl.semaphore_signal(barrier, inc=1, device_id=(row, peer(d)), device_id_type=MESH)
    for dev in (z_up, z_dn, x_near):
        pl.semaphore_signal(barrier, inc=1, device_id=dev, device_id_type=MESH)

    amps = pltpu.make_async_copy(x_ref, xbuf, loc.at[0])
    amps.start()
    mine = pltpu.make_async_copy(w_ref, wbuf.at[xh * 4 + y, core], loc.at[1])
    mine.start()

    sends = []
    waiting = []
    in_flight = {}

    def push(src, dst, rsem, dev, way=None):
        queue = in_flight.setdefault(way, [])
        if way is not None and len(queue) == DEPTH:
            queue.pop(0).wait_send()
        cp = pltpu.make_async_remote_copy(
            src_ref=src, dst_ref=dst, send_sem=ss.at[len(sends)], recv_sem=rsem,
            device_id=dev, device_id_type=MESH)
        cp.start()
        sends.append(cp)
        queue.append(cp)

    def arrived(ref, rsem):
        pltpu.make_async_remote_copy(
            src_ref=ref, dst_ref=ref, send_sem=ss.at[N_SENDS - 1], recv_sem=rsem,
            device_id=sibling, device_id_type=MESH).wait_recv()

    def wslot(da, db, j):
        return wbuf.at[((xh + da) % 2) * 4 + (y + 4 + sgn * db) % 4, core, pl.ds(j * PART, PART)]

    def trows(j):
        return pl.multiple_of(((xh + j // 2) % 2) * 512 + ((y // 2 + j % 2) % 2) * 256, 256)

    def tslot(da, db, j):
        return tbuf.at[((z + 4 + sgn * db) % 4) * 2 + (xl + da) % 2, pl.ds(trows(j), PART)]

    def send(op, da, db, j):
        slot, sems = (wslot, w_rs) if op[0] == "w" else (tslot, t_rs)
        dev, da2, db2 = {
            "w_up": (y_up, da, db + 3), "w_dn": (y_dn, da, db + 1), "w_far": (x_far, 1 - da, db),
            "t_up": (z_up, da, db + 3), "t_dn": (z_dn, da, db + 1), "t_near": (x_near, 1 - da, db),
        }[op]
        ref = slot(da, db, j)
        way = "x" if op in ("w_far", "t_near") else op
        push(ref, ref, sems.at[da2, db2 % 4, j], dev, way)

    def share(da, db, j):
        ref = wslot(da, db, j)
        push(ref, ref, s_rs.at[da, db, j], sibling)
        waiting.append((da, db, j))

    def w_in(da, db, j):
        arrived(wslot(da, db, j), w_rs.at[da, db, j])
        share(da, db, j)

    def t_in(da, db, j):
        if (da, db) != (0, 0):
            arrived(tslot(da, db, j), t_rs.at[da, db, j])
            return
        a = (xh + j // 2) % 2
        for i in range(2):
            for k in range(2):
                b = ((y // 2 + j % 2) % 2) * 2 + (y + i) % 2
                if (j, i, k) != (0, 0, 0):
                    c = col_of(a, b, (core + k) % 2)
                    arrived(piece(c), a_rs.at[c])

    def shared(da, db, j):
        ref = wbuf.at[((xh + da) % 2) * 4 + (y + 4 - sgn * db) % 4, 1 - core, pl.ds(j * PART, PART)]
        arrived(ref, s_rs.at[da, db, j])

    def piece(c):
        return tbuf.at[row, pl.ds(pl.multiple_of(c * 64, 64), 64)]

    amps.wait()

    rid = lax.broadcasted_iota(jnp.int32, (64, 128), 0)
    lane = lax.broadcasted_iota(jnp.int32, (64, 128), 1)
    live_src = (rid % OCC < nocc[row]) & (col * 4 + rid // OCC < nvirt[row ^ g])

    def prepare(h2, _):
        for p in range(OCC):
            s32[pl.ds(p, 64, stride=OCC), 0:VIR] = xbuf[h2, p].astype(jnp.float32)
        for pair in range(8):
            lo = s32[pl.ds(pair * 128, 64), :]
            hi = pltpu.roll(s32[pl.ds(pair * 128 + 64, 64), :], 64, 1)
            both = jnp.where(live_src, jnp.where(lane < VIR, lo, hi), 0.0)
            lhs[pl.ds(h2 * 64, 64), pl.ds(pair * 128, 128)] = both.astype(jnp.bfloat16)
        return 0

    lax.fori_loop(0, NIRREP, prepare, 0)
    mine.wait()
    pl.semaphore_wait(barrier, len(others) + 3)
    for op in FIRST:
        send(*op)
    for j in range(4):
        share(0, 0, j)

    src = lax.broadcasted_iota(jnp.int32, (1024, 256), 0)
    dst = lax.broadcasted_iota(jnp.int32, (1024, 256), 1)
    code = (src % VIR) * OCC + src // VIR
    for n in range(4):
        onehot = jnp.where(code == dst + n * 256, 1.0, 0.0).astype(jnp.bfloat16)
        moved = jnp.dot(lhs[...], onehot, preferred_element_type=jnp.float32).astype(jnp.bfloat16)
        for h2 in range(NIRREP):
            abuf[h2 * 2 + n // 2, :, (n % 2) * 256:(n % 2) * 256 + 256] = moved[h2 * 64:h2 * 64 + 64, :]

    for d in others:
        push(abuf.at[peer(d)], piece(col), a_rs.at[col], (row, peer(d)))
    tbuf[row, pl.ds(pl.multiple_of(col * 64, 64), 64), :] = abuf[col]

    h2 = col // 2
    jj = lax.broadcasted_iota(jnp.int32, (OCC, BLOCK), 1)
    ii = lax.broadcasted_iota(jnp.int32, (OCC, BLOCK), 0)
    c_occ = jnp.zeros((OCC, BLOCK), jnp.float32)
    r_occ = jnp.zeros((OCC, BLOCK), jnp.float32)
    for p in range(OCC):
        c_occ = jnp.where(jj % OCC == p, eocc[h2, p], c_occ)
        r_occ = jnp.where(ii == p, eocc[row, p], r_occ)
    c_vir = jnp.zeros((OCC, BLOCK), jnp.float32)
    for q in range(32):
        c_vir = jnp.where(jj // OCC == q, evirt[h2 ^ g, core * 32 + q], c_vir)
    c_e = c_occ - c_vir
    ok = (jj % OCC < nocc[h2]) & (core * 32 + jj // OCC < nvirt[h2 ^ g]) & (ii < nocc[row])
    n_row = nvirt[row ^ g]

    def factor(q, _):
        e = (r_occ - evirt[row ^ g, q]) + c_e
        inv[pl.ds(pl.multiple_of(q * OCC, OCC), OCC), :] = jnp.where(ok & (q < n_row), 1.0 / e, 0.0)
        return 0

    lax.fori_loop(0, VIR, factor, 0)
    acc[...] = jnp.zeros_like(acc)

    def part(h, rows):
        return (jnp.dot(wbuf[h, 0, rows, :], tbuf[h, 0:512, :], preferred_element_type=jnp.float32)
                + jnp.dot(wbuf[h, 1, rows, :], tbuf[h, 512:1024, :], preferred_element_type=jnp.float32))

    def product(h, m):
        rows = pl.ds(m * TILE, TILE)
        acc[rows, :] += part(h, rows)

    def rank(da, db):
        dist = (db * (4 - db) + 2) // 3
        return da * (2 + dist) + (1 - da) * (dist // 2)

    def stage_of(da, db):
        d = min(db, 4 - db)
        return 2 + d if da else d // 2

    last_w = (1 - xh) * 4 + (y + 2) % 4
    last_t = ((z + 2) % 4) * 2 + 1 - xl

    def products(stage, m):
        for key in [k for k in waiting if stage_of(*k[:2]) <= stage]:
            waiting.remove(key)
            shared(*key)

        def each(h, _):
            by_w = rank((h // 4 + xh) % 2, (h % 4 + 4 - y) % 4)
            by_t = rank((h % 2 + xl) % 2, (h // 2 + 4 - z) % 4)

            @pl.when((by_w <= stage) & (by_t <= stage) & ((by_w == stage) | (by_t == stage)))
            def _():
                product(h, m)
            return 0

        lax.fori_loop(0, NIRREP, each, 0)

    def quarter(j):

        @pl.when(last_w != last_t)
        def _():
            cols = pl.ds(pl.multiple_of(((y // 2 + j % 2) % 2) * 256, 256), 256)
            for m in range(ROWS // TILE):
                rows = pl.ds(m * TILE, TILE)
                acc[rows, :] += jnp.dot(wbuf[last_t, (xh + j // 2) % 2, rows, cols],
                                        tbuf[last_t, pl.ds(trows(j), PART), :],
                                        preferred_element_type=jnp.float32)

    def finish(da, db, j):
        waiting.remove((da, db, j))
        shared(da, db, j)
        rows = pl.ds(j * PART, PART)
        acc[rows, :] = (acc[rows, :] + part(last_w, rows)) * inv[rows, :]

    final = [op for op in ORDER if op[0] == "w_in" and op[1:3] == (1, 2)]
    for op in ORDER:
        if op in FIRST:
            continue
        if op[0] == "prod":
            products(*op[1:])
        elif op[0] == "w_in":
            w_in(*op[1:])
        elif op[0] == "t_in":
            t_in(*op[1:])
        else:
            send(*op)
    for j in range(4):
        quarter(j)
    for i, op in enumerate(final):
        finish(*op[1:])
    for queue in in_flight.values():
        for cp in queue:
            cp.wait_send()


def per_device(t2_pairs, cycle_ints, eps_occ, eps_virt, occ_count, virt_count, window_irrep):
    amps = t2_pairs.reshape(NIRREP, OCC, OCC * t2_pairs.shape[4], VIR)
    hbm = pl.BlockSpec(memory_space=pl.ANY)
    vmem = pl.BlockSpec(memory_space=pltpu.VMEM)
    smem = pl.BlockSpec(memory_space=pltpu.SMEM)
    return pl.pallas_call(
        kernel,
        out_shape=pltpu.VMEM((ROWS, BLOCK), jnp.float32),
        in_specs=[hbm, hbm, smem, smem, smem, smem, smem],
        out_specs=vmem,
        scratch_shapes=[
            pltpu.VMEM((NIRREP, OCC, 64, VIR), jnp.bfloat16),
            pltpu.VMEM((NIRREP, 2, ROWS, BLOCK), jnp.bfloat16),
            pltpu.VMEM((NIRREP, ROWS, BLOCK), jnp.bfloat16),
            pltpu.VMEM((16, 64, BLOCK), jnp.bfloat16),
            pltpu.VMEM((1024, 128), jnp.float32),
            pltpu.VMEM((512, 1024), jnp.bfloat16),
            pltpu.VMEM((ROWS, BLOCK), jnp.float32),
            pltpu.SemaphoreType.DMA((2, 4, 4)),
            pltpu.SemaphoreType.DMA((2, 4, 4)),
            pltpu.SemaphoreType.DMA((2, 4, 4)),
            pltpu.SemaphoreType.DMA((16,)),
            pltpu.SemaphoreType.DMA((N_SENDS,)),
            pltpu.SemaphoreType.DMA((2,)),
        ],
        compiler_params=pltpu.CompilerParams(
            collective_id=0, has_side_effects=True, vmem_limit_bytes=58 << 20),
    )(amps, cycle_ints, eps_occ, eps_virt, occ_count, virt_count, window_irrep)


def solution(mesh):
    placed = (P("row", None, None, None, "col", None), P("row", "col"), P(), P(), P(), P(), P())
    return jax.shard_map(
        per_device, mesh=mesh, in_specs=placed, out_specs=P("row", "col"), check_vma=False
    )
```

```python
import jax
import jax.numpy as jnp
from jax import lax
from jax.experimental import pallas as pl
from jax.experimental.pallas import tpu as pltpu
from jax.sharding import PartitionSpec as P

MESH = pl.DeviceIdType.MESH
NIRREP = 8
OCC = 16
VIR = 64
BLOCK = 512
ROWS = 1024
PART = 256
TILE = 512
N_SENDS = 110
DEPTH = 3
FIRST = [("w_up", 0, 0, 0), ("w_dn", 0, 0, 2), ("w_far", 0, 0, 0)]
ORDER = [
    ("w_up", 0, 0, 0), ("w_dn", 0, 0, 2), ("w_far", 0, 0, 0), ("w_up", 0, 0, 1), ("w_dn", 0, 0, 3),
    ("w_in", 0, 3, 0), ("w_in", 0, 1, 2), ("w_in", 1, 0, 0), ("t_in", 0, 0, 0), ("t_up", 0, 0, 0),
    ("t_dn", 0, 0, 0), ("t_near", 0, 0, 0), ("t_in", 0, 0, 1), ("t_up", 0, 0, 1),
    ("t_dn", 0, 0, 1), ("w_up", 0, 0, 2), ("w_dn", 0, 0, 0), ("w_far", 0, 0, 2), ("t_in", 0, 0, 2),
    ("t_up", 0, 0, 2), ("t_dn", 0, 0, 2), ("t_in", 0, 3, 0), ("t_in", 0, 1, 0), ("t_in", 0, 0, 3),
    ("t_up", 0, 0, 3), ("t_dn", 0, 0, 3), ("w_up", 0, 0, 3), ("w_dn", 0, 0, 1),
    ("t_near", 0, 0, 1), ("t_in", 0, 3, 1), ("t_in", 0, 1, 1), ("w_in", 0, 3, 1),
    ("w_in", 0, 1, 3), ("t_in", 1, 0, 0), ("t_up", 0, 3, 0), ("w_up", 0, 3, 0), ("w_dn", 0, 1, 2),
    ("w_far", 0, 0, 1), ("t_in", 0, 3, 2), ("t_in", 0, 1, 2), ("t_dn", 0, 1, 2), ("w_in", 0, 3, 2),
    ("w_in", 0, 1, 0), ("w_in", 1, 0, 2), ("t_up", 0, 3, 1), ("w_up", 0, 3, 1), ("w_dn", 0, 1, 3),
    ("t_near", 0, 0, 2), ("t_in", 0, 3, 3), ("t_in", 0, 1, 3), ("t_dn", 0, 1, 3),
    ("w_in", 0, 3, 3), ("w_in", 0, 1, 1), ("t_in", 1, 0, 1), ("t_up", 1, 0, 0), ("t_dn", 1, 0, 0),
    ("w_up", 1, 0, 0), ("w_dn", 1, 0, 2), ("w_far", 0, 0, 3), ("prod", 0, 0), ("t_in", 0, 2, 0),
    ("t_in", 0, 2, 2), ("w_in", 0, 2, 0), ("w_in", 0, 2, 2), ("w_in", 1, 0, 1), ("prod", 0, 1),
    ("t_up", 1, 0, 1), ("t_dn", 1, 0, 1), ("w_up", 1, 0, 2), ("w_dn", 1, 0, 0),
    ("t_near", 0, 0, 3), ("t_in", 0, 2, 1), ("t_in", 0, 2, 3), ("w_in", 0, 2, 1),
    ("w_in", 0, 2, 3), ("t_in", 1, 0, 2), ("t_up", 1, 0, 2), ("t_dn", 1, 0, 2), ("w_up", 1, 0, 1),
    ("t_near", 0, 2, 1), ("prod", 1, 0), ("t_in", 1, 3, 0), ("t_in", 1, 1, 0), ("w_in", 1, 3, 0),
    ("w_in", 1, 1, 2), ("w_in", 1, 0, 3), ("w_dn", 1, 0, 3), ("prod", 1, 1), ("w_up", 1, 0, 3),
    ("w_dn", 1, 0, 1), ("w_far", 0, 2, 1), ("t_in", 1, 3, 1), ("t_in", 1, 1, 1), ("w_in", 1, 3, 2),
    ("w_in", 1, 1, 0), ("t_in", 1, 0, 3), ("t_up", 1, 0, 3), ("t_dn", 1, 0, 3), ("t_up", 1, 3, 0),
    ("w_up", 1, 3, 0), ("w_far", 0, 2, 2), ("prod", 2, 0), ("t_in", 1, 3, 2), ("t_in", 1, 1, 2),
    ("t_dn", 1, 1, 2), ("w_in", 1, 3, 1), ("w_in", 1, 1, 3), ("t_in", 1, 2, 1), ("w_dn", 1, 1, 3),
    ("prod", 2, 1), ("t_in", 1, 3, 3), ("t_in", 1, 1, 3), ("t_dn", 1, 1, 3), ("w_in", 1, 3, 3),
    ("w_in", 1, 1, 1), ("w_in", 1, 2, 1), ("prod", 3, 0), ("t_in", 1, 2, 0), ("t_in", 1, 2, 2),
    ("w_in", 1, 2, 0), ("w_in", 1, 2, 3), ("w_in", 1, 2, 2), ("prod", 3, 1), ("t_in", 1, 2, 3),
]


def kernel(x_ref, w_ref, eocc, evirt, nocc, nvirt, window, acc, inv, w_last, t_last, xbuf, wbuf, tbuf, abuf, s32, lhs,
           w_rs, s_rs, t_rs, a_rs, ss, loc):
    row = lax.axis_index("row")
    col = lax.axis_index("col")
    z, xl = row // 2, row % 2
    xh, y, core = col // 8, (col // 2) % 4, col % 2
    sgn = 1 - 2 * core
    g = window[0]

    def col_of(a, b, k):
        return a * 8 + b * 2 + k

    y_up = (row, col_of(xh, (y + 4 + sgn) % 4, core))
    y_dn = (row, col_of(xh, (y + 4 - sgn) % 4, core))
    x_far = (row, col_of(1 - xh, y, core))
    sibling = (row, col_of(xh, y, 1 - core))
    z_up = (((z + 4 + sgn) % 4) * 2 + xl, col)
    z_dn = (((z + 4 - sgn) % 4) * 2 + xl, col)
    x_near = (z * 2 + 1 - xl, col)
    others = [(dx, dy, dk) for dx in range(2) for dy in (0, 1, 3, 2) for dk in range(2)
              if (dx, dy, dk) != (0, 0, 0)]

    def peer(d):
        return col_of((xh + d[0]) % 2, (y + d[1]) % 4, (core + d[2]) % 2)

    barrier = pltpu.get_barrier_semaphore()
    for d in others:
        pl.semaphore_signal(barrier, inc=1, device_id=(row, peer(d)), device_id_type=MESH)
    for dev in (z_up, z_dn, x_near):
        pl.semaphore_signal(barrier, inc=1, device_id=dev, device_id_type=MESH)

    amps = pltpu.make_async_copy(x_ref, xbuf, loc.at[0])
    amps.start()
    mine = pltpu.make_async_copy(w_ref, wbuf.at[xh * 4 + y, core], loc.at[1])
    mine.start()

    sends = []
    waiting = []
    in_flight = {}

    def push(src, dst, rsem, dev, way=None):
        queue = in_flight.setdefault(way, [])
        if way is not None and len(queue) == DEPTH:
            queue.pop(0).wait_send()
        cp = pltpu.make_async_remote_copy(
            src_ref=src, dst_ref=dst, send_sem=ss.at[len(sends)], recv_sem=rsem,
            device_id=dev, device_id_type=MESH)
        cp.start()
        sends.append(cp)
        queue.append(cp)

    def arrived(ref, rsem):
        pltpu.make_async_remote_copy(
            src_ref=ref, dst_ref=ref, send_sem=ss.at[N_SENDS - 1], recv_sem=rsem,
            device_id=sibling, device_id_type=MESH).wait_recv()

    def wslot(da, db, j):
        if (da, db) == (1, 2):
            return w_last.at[core, pl.ds(j * PART, PART)]
        return wbuf.at[((xh + da) % 2) * 4 + (y + 4 + sgn * db) % 4, core, pl.ds(j * PART, PART)]

    def trows(j):
        return pl.multiple_of(((xh + j // 2) % 2) * 512 + ((y // 2 + j % 2) % 2) * 256, 256)

    def tslot(da, db, j):
        return tbuf.at[((z + 4 + sgn * db) % 4) * 2 + (xl + da) % 2, pl.ds(trows(j), PART)]

    def send(op, da, db, j):
        slot, sems = (wslot, w_rs) if op[0] == "w" else (tslot, t_rs)
        dev, da2, db2 = {
            "w_up": (y_up, da, db + 3), "w_dn": (y_dn, da, db + 1), "w_far": (x_far, 1 - da, db),
            "t_up": (z_up, da, db + 3), "t_dn": (z_dn, da, db + 1), "t_near": (x_near, 1 - da, db),
        }[op]
        ref = slot(da, db, j)
        there = ref
        if slot is wslot and (da2, db2 % 4) == (1, 2):
            there = w_last.at[core, pl.ds(j * PART, PART)]
        way = "x" if op in ("w_far", "t_near") else op
        push(ref, there, sems.at[da2, db2 % 4, j], dev, way)

    def share(da, db, j):
        ref = wslot(da, db, j)
        push(ref, ref, s_rs.at[da, db, j], sibling)
        waiting.append((da, db, j))

    def w_in(da, db, j):
        arrived(wslot(da, db, j), w_rs.at[da, db, j])
        share(da, db, j)

    def t_in(da, db, j):
        if (da, db) != (0, 0):
            arrived(tslot(da, db, j), t_rs.at[da, db, j])
            return
        a = (xh + j // 2) % 2
        for i in range(2):
            for k in range(2):
                b = ((y // 2 + j % 2) % 2) * 2 + (y + i) % 2
                if (j, i, k) != (0, 0, 0):
                    c = col_of(a, b, (core + k) % 2)
                    arrived(piece(c), a_rs.at[c])

    def shared(da, db, j):
        ref = w_last.at[1 - core, pl.ds(j * PART, PART)] if (da, db) == (1, 2) else wbuf.at[((xh + da) % 2) * 4 + (y + 4 - sgn * db) % 4, 1 - core, pl.ds(j * PART, PART)]
        arrived(ref, s_rs.at[da, db, j])

    def piece(c):
        return tbuf.at[row, pl.ds(pl.multiple_of(c * 64, 64), 64)]

    amps.wait()

    rid = lax.broadcasted_iota(jnp.int32, (64, 128), 0)
    lane = lax.broadcasted_iota(jnp.int32, (64, 128), 1)
    live_src = (rid % OCC < nocc[row]) & (col * 4 + rid // OCC < nvirt[row ^ g])

    def prepare(h2, _):
        for p in range(OCC):
            s32[pl.ds(p, 64, stride=OCC), 0:VIR] = xbuf[h2, p].astype(jnp.float32)
        for pair in range(8):
            lo = s32[pl.ds(pair * 128, 64), :]
            hi = pltpu.roll(s32[pl.ds(pair * 128 + 64, 64), :], 64, 1)
            both = jnp.where(live_src, jnp.where(lane < VIR, lo, hi), 0.0)
            lhs[pl.ds(h2 * 64, 64), pl.ds(pair * 128, 128)] = both.astype(jnp.bfloat16)
        return 0

    lax.fori_loop(0, NIRREP, prepare, 0)
    mine.wait()
    pl.semaphore_wait(barrier, len(others) + 3)
    for op in FIRST:
        send(*op)
    for j in range(4):
        share(0, 0, j)

    src = lax.broadcasted_iota(jnp.int32, (1024, 256), 0)
    dst = lax.broadcasted_iota(jnp.int32, (1024, 256), 1)
    code = (src % VIR) * OCC + src // VIR
    for n in range(4):
        onehot = jnp.where(code == dst + n * 256, 1.0, 0.0).astype(jnp.bfloat16)
        moved = jnp.dot(lhs[...], onehot, preferred_element_type=jnp.float32).astype(jnp.bfloat16)
        for h2 in range(NIRREP):
            abuf[h2 * 2 + n // 2, :, (n % 2) * 256:(n % 2) * 256 + 256] = moved[h2 * 64:h2 * 64 + 64, :]

    for d in others:
        push(abuf.at[peer(d)], piece(col), a_rs.at[col], (row, peer(d)))
    tbuf[row, pl.ds(pl.multiple_of(col * 64, 64), 64), :] = abuf[col]

    h2 = col // 2
    jj = lax.broadcasted_iota(jnp.int32, (OCC, BLOCK), 1)
    ii = lax.broadcasted_iota(jnp.int32, (OCC, BLOCK), 0)
    c_occ = jnp.zeros((OCC, BLOCK), jnp.float32)
    r_occ = jnp.zeros((OCC, BLOCK), jnp.float32)
    for p in range(OCC):
        c_occ = jnp.where(jj % OCC == p, eocc[h2, p], c_occ)
        r_occ = jnp.where(ii == p, eocc[row, p], r_occ)
    c_vir = jnp.zeros((OCC, BLOCK), jnp.float32)
    for q in range(32):
        c_vir = jnp.where(jj // OCC == q, evirt[h2 ^ g, core * 32 + q], c_vir)
    c_e = c_occ - c_vir
    ok = (jj % OCC < nocc[h2]) & (core * 32 + jj // OCC < nvirt[h2 ^ g]) & (ii < nocc[row])
    n_row = nvirt[row ^ g]

    def factor(q, _):
        e = (r_occ - evirt[row ^ g, q]) + c_e
        inv[pl.ds(pl.multiple_of(q * OCC, OCC), OCC), :] = jnp.where(ok & (q < n_row), 1.0 / e, 0.0)
        return 0

    lax.fori_loop(0, VIR, factor, 0)
    acc[...] = jnp.zeros_like(acc)

    def part(h, rows):
        return (jnp.dot(wbuf[h, 0, rows, :], tbuf[h, 0:512, :], preferred_element_type=jnp.float32)
                + jnp.dot(wbuf[h, 1, rows, :], tbuf[h, 512:1024, :], preferred_element_type=jnp.float32))

    def product(h, m):
        rows = pl.ds(m * TILE, TILE)
        acc[rows, :] += part(h, rows)

    def rank(da, db):
        dist = (db * (4 - db) + 2) // 3
        return da * (2 + dist) + (1 - da) * (dist // 2)

    def stage_of(da, db):
        d = min(db, 4 - db)
        return 2 + d if da else d // 2

    last_w = (1 - xh) * 4 + (y + 2) % 4
    last_t = ((z + 2) % 4) * 2 + 1 - xl

    def products(stage, m):
        for key in [k for k in waiting if stage_of(*k[:2]) <= stage]:
            waiting.remove(key)
            shared(*key)

        def each(h, _):
            by_w = rank((h // 4 + xh) % 2, (h % 4 + 4 - y) % 4)
            by_t = rank((h % 2 + xl) % 2, (h // 2 + 4 - z) % 4)

            @pl.when((by_w <= stage) & (by_t <= stage) & ((by_w == stage) | (by_t == stage)))
            def _():
                product(h, m)
            return 0

        lax.fori_loop(0, NIRREP, each, 0)

    def quarter(j):

        @pl.when(last_w != last_t)
        def _():
            cols = pl.ds(pl.multiple_of(((y // 2 + j % 2) % 2) * 256, 256), 256)
            for m in range(ROWS // TILE):
                rows = pl.ds(m * TILE, TILE)
                acc[rows, :] += jnp.dot(wbuf[last_t, (xh + j // 2) % 2, rows, cols],
                                        tbuf[last_t, pl.ds(trows(j), PART), :],
                                        preferred_element_type=jnp.float32)

    final = [op for op in ORDER if op[0] == "w_in" and op[1:3] == (1, 2)]
    for op in ORDER:
        if op in FIRST:
            continue
        if op[0] == "prod":
            products(*op[1:])
        elif op[0] == "w_in":
            w_in(*op[1:])
        elif op[0] == "t_in":
            t_in(*op[1:])
        else:
            send(*op)
    keep = pltpu.make_async_copy(tbuf.at[last_w], t_last, loc.at[0])
    keep.start()
    for j in range(4):
        quarter(j)
    for op in final:
        shared(*op[1:])
    keep.wait()
    for queue in in_flight.values():
        for cp in queue:
            cp.wait_send()


def deliver(acc, inv, w_last, t_last, out_ref, done, sems):
    copies = []
    for i in range(ROWS // PART):
        rows = pl.ds(i * PART, PART)
        total = jnp.dot(w_last[0, rows, :], t_last[0:512, :], preferred_element_type=jnp.float32)
        total += jnp.dot(w_last[1, rows, :], t_last[512:1024, :], preferred_element_type=jnp.float32)
        done[rows, :] = (acc[rows, :] + total) * inv[rows, :]
        cp = pltpu.make_async_copy(done.at[rows], out_ref.at[rows], sems.at[i])
        cp.start()
        copies.append(cp)
    for cp in copies:
        cp.wait()


def per_device(t2_pairs, cycle_ints, eps_occ, eps_virt, occ_count, virt_count, window_irrep):
    amps = t2_pairs.reshape(NIRREP, OCC, OCC * t2_pairs.shape[4], VIR)
    hbm = pl.BlockSpec(memory_space=pl.ANY)
    vmem = pl.BlockSpec(memory_space=pltpu.VMEM)
    smem = pl.BlockSpec(memory_space=pltpu.SMEM)
    parts = pl.pallas_call(
        kernel,
        out_shape=[pltpu.VMEM((ROWS, BLOCK), jnp.float32)] * 2 + [
            pltpu.VMEM((2, ROWS, BLOCK), jnp.bfloat16), pltpu.VMEM((ROWS, BLOCK), jnp.bfloat16)],
        in_specs=[hbm, hbm, smem, smem, smem, smem, smem],
        out_specs=[vmem] * 4,
        scratch_shapes=[
            pltpu.VMEM((NIRREP, OCC, 64, VIR), jnp.bfloat16),
            pltpu.VMEM((NIRREP, 2, ROWS, BLOCK), jnp.bfloat16),
            pltpu.VMEM((NIRREP, ROWS, BLOCK), jnp.bfloat16),
            pltpu.VMEM((16, 64, BLOCK), jnp.bfloat16),
            pltpu.VMEM((1024, 128), jnp.float32),
            pltpu.VMEM((512, 1024), jnp.bfloat16),
            pltpu.SemaphoreType.DMA((2, 4, 4)),
            pltpu.SemaphoreType.DMA((2, 4, 4)),
            pltpu.SemaphoreType.DMA((2, 4, 4)),
            pltpu.SemaphoreType.DMA((16,)),
            pltpu.SemaphoreType.DMA((N_SENDS,)),
            pltpu.SemaphoreType.DMA((2,)),
        ],
        compiler_params=pltpu.CompilerParams(
            collective_id=0, has_side_effects=True, vmem_limit_bytes=48 << 20),
    )(amps, cycle_ints, eps_occ, eps_virt, occ_count, virt_count, window_irrep)
    return pl.pallas_call(
        deliver,
        out_shape=jax.ShapeDtypeStruct((ROWS, BLOCK), jnp.float32),
        in_specs=[vmem] * 4,
        out_specs=hbm,
        scratch_shapes=[
            pltpu.VMEM((ROWS, BLOCK), jnp.float32),
            pltpu.SemaphoreType.DMA((ROWS // PART,)),
        ],
        compiler_params=pltpu.CompilerParams(vmem_limit_bytes=6 << 20),
    )(*parts)


def solution(mesh):
    placed = (P("row", None, None, None, "col", None), P("row", "col"), P(), P(), P(), P(), P())
    return jax.shard_map(
        per_device, mesh=mesh, in_specs=placed, out_specs=P("row", "col"), check_vma=False
    )
```
